32 devices in a mesh: replica: 2 (over x), fsdp: 4 (over y, core), tensor: 4 (over z).
Axes of the slice: x: 2, y: 2, z: 4, core: 2. Of those that a mesh axis runs over, the one named last changes fastest.
Arguments:
- tokens: bfloat16 [2, 2048, 5376], P(None, ('replica', 'fsdp', 'tensor')), may hold values from -6 to 6
- key_cot: bfloat16 [2, 2048, 512], P(None, ('replica', 'fsdp'), 'tensor'), may hold values from -6 to 6
- key_master: float32 [2, 5376, 512], P('replica', 'fsdp', 'tensor'), may hold values from -6 to 6
- adam_first: float32 [2, 5376, 512], P('replica', 'fsdp', 'tensor'), may hold values from -6 to 6
- adam_second: float32 [2, 5376, 512], P('replica', 'fsdp', 'tensor'), may hold values from 0.25 to 4
- frag_local: float32 [2, 8, 2, 5376, 512], P('replica', None, None, 'fsdp', 'tensor'), may hold values from -6 to 6
- frag_global: float32 [8, 2, 5376, 512], P(None, None, 'fsdp', 'tensor'), may hold values from -6 to 6
- frag_moment: float32 [8, 2, 5376, 512], P(None, None, 'fsdp', 'tensor'), may hold values from -3 to 3
- frag_order: int32 [8], replicated, may hold values from 0 to 7, each once
Outputs:
- keys: bfloat16 [2, 2048, 512], P(None, ('replica', 'fsdp'), 'tensor')
- new_master: float32 [2, 5376, 512], P('replica', 'fsdp', 'tensor')
- new_first: float32 [2, 5376, 512], P('replica', 'fsdp', 'tensor')
- new_second: float32 [2, 5376, 512], P('replica', 'fsdp', 'tensor')
- new_global: float32 [2, 5376, 512], P(None, 'fsdp', 'tensor')
- new_moment: float32 [2, 5376, 512], P(None, 'fsdp', 'tensor')
- mixed_local: float32 [2, 2, 5376, 512], P('replica', None, 'fsdp', 'tensor')
The draws below stay inside these ranges and needn't reach their ends.
Inputs may be any that keep to these rules, and one draw needn't show every extreme that they name: `frag_order`: each fragment appears once.
All inputs are finite; a program needn't handle non-finite values.
Results may differ from the reference program's by a relative error of at most 0.0049.
Values may be sent and summed in bfloat16 or wider, within the bound.
No kernel may reach another device: no remote copies, remote signals or barrier semaphores. Data moves between devices by JAX's collectives and lax.ppermute only.
A program may use at most 128 MiB of HBM per device.

```python
import math
import jax
import jax.numpy as jnp
from jax import lax

D = 5376
C = 512
MICRO = 2
FRAGS = 8
FL = 2
TOKENS = 2048
N_REPLICA = 2


def strengthened(drawn, key, source, target, blocks, factor):
    def block_of(axis_at):
        return (jnp.arange(drawn.shape[axis_at]) // (drawn.shape[axis_at] // blocks)).reshape((-1,) + (1,) * (drawn.ndim - 1 - axis_at))

    first = jax.random.permutation(key, blocks)[block_of(target)]
    second = (block_of(target) + blocks // 2) % blocks
    return jnp.where((block_of(source) == first) | (block_of(source) == second), factor * drawn, drawn)


def shard_levels(rng, shape, cuts, low, top_value):
    factor_of = 1.0
    for axis_at, shards_of in cuts:
        heights = jax.random.uniform(jax.random.fold_in(jax.random.fold_in(rng, 6), axis_at), (shards_of,), jnp.float32, low / len(cuts), top_value / len(cuts))
        factor_of = factor_of * jnp.repeat(jnp.exp(heights), shape[axis_at] // shards_of).reshape((-1,) + (1,) * (len(shape) - 1 - axis_at))
    return factor_of


def scatter_about(own_key, shape, spread, bound, cuts=(), dtype=jnp.bfloat16):
    drawn = jax.random.normal(own_key, shape, jnp.float32) * spread
    if len(cuts) > 0:
        drawn = shard_levels(own_key, shape, cuts, -0.22, 0.18) * drawn
    return jnp.clip(drawn, min=-bound, max=bound).astype(dtype)


def gaussian_with(stream_key, dims, width, reach, pieces, heavy, kind=jnp.bfloat16):
    drawn = width * jax.random.normal(stream_key, dims, jnp.float32)
    if pieces:
        drawn = drawn * shard_levels(stream_key, dims, pieces, -0.22, 0.18)
    return jnp.clip(strengthened(drawn, jax.random.fold_in(stream_key, 3), *heavy), -reach, reach).astype(kind)


def setup_inputs(seed: int = 0) -> dict:
    splits = jax.random.split(jax.random.key(seed), 10)
    return {
        "tokens": gaussian_with(splits[0], (MICRO, TOKENS, D), 1.0, 6.0, ((1, 32),), (1, 2, 32, 2.75)),
        "key_cot": scatter_about(splits[1], (MICRO, TOKENS, C), 1.0, 6.0, ((1, 8), (2, 4))),
        "key_master": scatter_about(splits[2], (N_REPLICA, D, C), 1.0, 6.0, ((0, 2), (1, 4), (2, 4)), jnp.float32),
        "adam_first": scatter_about(splits[3], (N_REPLICA, D, C), 1.0, 6.0, ((0, 2), (1, 4), (2, 4)), jnp.float32),
        "adam_second": jnp.clip(jnp.exp(math.log(4.0) - 2.7725887 * jax.random.uniform(splits[4], (N_REPLICA, D, C), jnp.float32) ** shard_levels(splits[4], (N_REPLICA, D, C), ((0, 2), (1, 4), (2, 4)), -0.2, 0.2)), 0.25, 4.0),
        "frag_local": scatter_about(splits[5], (N_REPLICA, FRAGS, FL, D, C), 1.0, 6.0, ((0, 2), (3, 4), (4, 4)), jnp.float32),
        "frag_global": scatter_about(splits[6], (FRAGS, FL, D, C), 1.0, 6.0, ((2, 4), (3, 4)), jnp.float32),
        "frag_moment": scatter_about(splits[7], (FRAGS, FL, D, C), 0.5, 3.0, ((2, 4), (3, 4)), jnp.float32),
        "frag_order": jax.random.permutation(splits[8], FRAGS).astype(jnp.int32),
    }


def reference(tokens, key_cot, key_master, adam_first, adam_second, frag_local, frag_global, frag_moment, frag_order):
    factor = D ** (-0.5)
    weights_bf = key_master.astype(jnp.bfloat16)
    span = TOKENS // N_REPLICA
    key_blocks = []
    grad_blocks = []
    for replica in range(N_REPLICA):
        token_rows = tokens[:, replica * span:(replica + 1) * span].reshape(MICRO * span, D)
        cot_rows = key_cot[:, replica * span:(replica + 1) * span].reshape(MICRO * span, C)
        projected = factor * jnp.dot(token_rows, weights_bf[replica], preferred_element_type=jnp.float32)
        key_blocks.append(projected.astype(jnp.bfloat16).reshape(MICRO, span, C))
        summed = lax.dot_general(token_rows, cot_rows, (((0,), (0,)), ((), ())), preferred_element_type=jnp.float32)
        grad_blocks.append(factor * summed)
    keys = jnp.concatenate(key_blocks, 1)
    gradient = jnp.stack(grad_blocks)
    new_first = 0.9 * adam_first + 0.1 * gradient
    new_second = 0.95 * adam_second + 0.05 * gradient * gradient
    first_hat = new_first / (1.0 - 0.9 ** 10)
    second_hat = new_second / (1.0 - 0.95 ** 10)
    new_master = key_master - 0.01 * (first_hat / (jnp.sqrt(second_hat) + 1e-08) + 0.1 * key_master)
    chosen = frag_order[0]
    local_frag = lax.dynamic_index_in_dim(frag_local, chosen, 1, keepdims=False)
    global_frag = lax.dynamic_index_in_dim(frag_global, chosen, 0, keepdims=False)
    moment_frag = lax.dynamic_index_in_dim(frag_moment, chosen, 0, keepdims=False)
    drift = global_frag[None] - local_frag
    outer_grad = lax.optimization_barrier(jnp.sum(drift, 0)) / N_REPLICA
    new_moment = 0.9 * moment_frag + outer_grad
    new_global = global_frag - 0.7 * (outer_grad + 0.9 * new_moment)
    mixed_local = 0.5 * local_frag + 0.5 * new_global[None]
    return (keys, new_master, new_first, new_second, new_global, new_moment, mixed_local)
```

```python
import functools

import jax
import jax.numpy as jnp
from jax import lax
from jax.experimental import pallas as pl
from jax.experimental.pallas import tpu as pltpu
from jax.sharding import PartitionSpec as P


def swap(value, axis, bit):
    count = lax.axis_size(axis)
    return lax.ppermute(value, axis, [(i, i ^ bit) for i in range(count)])


def split_kernel(count, order, me_ref, tokens_ref, *piece_refs):
    width = tokens_ref.shape[2] // count
    me = me_ref[0]
    for distance, piece_ref in zip(order, piece_refs):
        for block in range(count):

            @pl.when(me == block ^ distance)
            def _(block=block, piece_ref=piece_ref):
                piece_ref[...] = tokens_ref[:, :, block * width : (block + 1) * width]


def split_features(tokens, axis, order):
    count = lax.axis_size(axis)
    micro_count, rows, features = tokens.shape
    piece = jax.ShapeDtypeStruct((micro_count, rows, features // count), tokens.dtype)
    return pl.pallas_call(
        functools.partial(split_kernel, count, order),
        out_shape=[piece] * len(order),
        in_specs=[
            pl.BlockSpec(memory_space=pltpu.SMEM),
            pl.BlockSpec(memory_space=pltpu.VMEM),
        ],
        out_specs=[pl.BlockSpec(memory_space=pltpu.VMEM)] * len(order),
        name="split_features",
    )(lax.axis_index(axis).reshape(1), tokens)


def project_by_swaps(tokens, key_cot, weights_bf):
    micro_count, rows, features = tokens.shape
    columns = key_cot.shape[2]
    f_count, t_count = lax.axis_size("fsdp"), lax.axis_size("tensor")
    t_index = lax.axis_index("tensor")
    factor = features ** (-0.5)

    f_order = [0]
    bit = f_count // 2
    while bit:
        f_order = f_order + [d | bit for d in f_order]
        bit //= 2

    pieces = dict(zip(f_order, split_features(tokens, "fsdp", f_order)))
    mine = {0: pieces[0]}
    for d in sorted(f_order[1:], reverse=True):
        mine[d] = swap(pieces[d], "fsdp", d)
    token_rows = jnp.concatenate([mine[d].reshape(micro_count * rows, -1) for d in f_order])

    cot_blocks = key_cot.reshape(micro_count, t_count, rows, columns)
    cots = []
    for d in range(t_count):
        block = lax.dynamic_index_in_dim(cot_blocks, t_index ^ d, 1, keepdims=False)
        cots.append(swap(block, "tensor", d) if d else block)
    cot_rows = jnp.concatenate([c.reshape(micro_count * rows, columns) for c in cots], 1)
    bit = f_count // 2
    while bit:
        cot_rows = jnp.concatenate([cot_rows, swap(cot_rows, "fsdp", bit)])
        bit //= 2

    weights = [weights_bf] + [swap(weights_bf, "tensor", d) for d in range(1, t_count)]

    partial = lax.dot_general(
        token_rows, cot_rows, (((0,), (0,)), ((), ())), preferred_element_type=jnp.float32
    )
    gradient = partial[:, :columns]
    for d in range(1, t_count):
        block = partial[:, d * columns : (d + 1) * columns].astype(jnp.bfloat16)
        gradient = gradient + swap(block, "tensor", d).astype(jnp.float32)
    gradient = factor * gradient

    summed = jnp.dot(
        token_rows, jnp.concatenate(weights, 1), preferred_element_type=jnp.float32
    )
    bit = 1
    while bit < f_count:
        half = summed.shape[0] // 2
        sent = summed[half:].astype(jnp.bfloat16)
        summed = summed[:half] + swap(sent, "fsdp", bit).astype(jnp.float32)
        bit *= 2
    keys_here = (factor * summed).astype(jnp.bfloat16).reshape(micro_count, rows, -1)
    blocks = []
    for d in range(t_count):
        block = keys_here[:, :, d * columns : (d + 1) * columns]
        blocks.append(swap(block, "tensor", d) if d else block)
    stacked = jnp.stack(blocks)
    keys = jnp.stack(
        [lax.dynamic_index_in_dim(stacked, t_index ^ t, 0, keepdims=False) for t in range(t_count)],
        1,
    ).reshape(micro_count, t_count * rows, columns)
    return keys, gradient


def project_by_gathers(tokens, key_cot, weights_bf):
    micro_count, _, features = tokens.shape
    columns = key_cot.shape[2]
    factor = features ** (-0.5)
    gathered = lax.all_gather(tokens, "tensor", axis=1, tiled=True)
    token_rows = gathered.reshape(-1, features)
    summed = jnp.dot(
        token_rows,
        lax.all_gather(weights_bf, "fsdp", axis=0, tiled=True),
        preferred_element_type=jnp.float32,
    )
    keys = (factor * summed).astype(jnp.bfloat16).reshape(micro_count, -1, columns)
    gradient = factor * lax.psum_scatter(
        lax.dot_general(
            token_rows,
            key_cot.reshape(-1, columns),
            (((0,), (0,)), ((), ())),
            preferred_element_type=jnp.float32,
        ),
        "fsdp",
        scatter_dimension=0,
        tiled=True,
    )
    return keys, gradient


def small_power_of_two(count):
    return count & (count - 1) == 0 and count <= 8


def on_device(
    tokens,
    key_cot,
    key_master,
    adam_first,
    adam_second,
    frag_local,
    frag_global,
    frag_moment,
    frag_order,
):
    master = key_master[0]
    weights_bf = master.astype(jnp.bfloat16)
    if small_power_of_two(lax.axis_size("fsdp")) and small_power_of_two(lax.axis_size("tensor")):
        keys, gradient = project_by_swaps(tokens, key_cot, weights_bf)
    else:
        keys, gradient = project_by_gathers(tokens, key_cot, weights_bf)

    chosen = frag_order[0]
    local_frag = lax.dynamic_index_in_dim(frag_local[0], chosen, 0, keepdims=False)
    global_frag = lax.dynamic_index_in_dim(frag_global, chosen, 0, keepdims=False)
    moment_frag = lax.dynamic_index_in_dim(frag_moment, chosen, 0, keepdims=False)
    drift = global_frag - local_frag
    replicas = lax.axis_size("replica")
    if replicas == 2:
        drift_sum = drift + swap(drift, "replica", 1)
    else:
        drift_sum = lax.psum(drift, "replica")
    outer_grad = drift_sum / replicas
    new_moment = 0.9 * moment_frag + outer_grad
    new_global = global_frag - 0.7 * (outer_grad + 0.9 * new_moment)
    mixed_local = 0.5 * local_frag + 0.5 * new_global

    new_first = 0.9 * adam_first[0] + 0.1 * gradient
    new_second = 0.95 * adam_second[0] + 0.05 * gradient * gradient
    first_hat = new_first / (1.0 - 0.9**10)
    second_hat = new_second / (1.0 - 0.95**10)
    new_master = master - 0.01 * (first_hat / (jnp.sqrt(second_hat) + 1e-08) + 0.1 * master)
    return (
        keys,
        new_master[None],
        new_first[None],
        new_second[None],
        new_global,
        new_moment,
        mixed_local[None],
    )


def solution(mesh):
    return jax.shard_map(
        on_device,
        mesh=mesh,
        in_specs=(
            P(None, ("replica", "fsdp", "tensor"), None),
            P(None, ("replica", "fsdp"), "tensor"),
            P("replica", "fsdp", "tensor"),
            P("replica", "fsdp", "tensor"),
            P("replica", "fsdp", "tensor"),
            P("replica", None, None, "fsdp", "tensor"),
            P(None, None, "fsdp", "tensor"),
            P(None, None, "fsdp", "tensor"),
            P(),
        ),
        out_specs=(
            P(None, ("replica", "fsdp"), "tensor"),
            P("replica", "fsdp", "tensor"),
            P("replica", "fsdp", "tensor"),
            P("replica", "fsdp", "tensor"),
            P(None, "fsdp", "tensor"),
            P(None, "fsdp", "tensor"),
            P("replica", None, "fsdp", "tensor"),
        ),
        check_vma=False,
    )
```
